128 devices in a mesh: col: 4 (over z), rhs: 32 (over x, y, core).
Axes of the slice: x: 4, y: 4, z: 4, core: 2. Of those that a mesh axis runs over, the one named last changes fastest.
Arguments:
- desc_rows: bfloat16 [128, 4096, 1024], P(('col', 'rhs')), may hold values from -6 to 6
- upd_factor: bfloat16 [128, 1024, 1024], P(('col', 'rhs')), may hold values from -0.03125 to 0.03125
- update_index: int32 [128, 1024], P(('col', 'rhs')), may hold values from -1 to 1023, as said below
- owner_map: int32 [128, 4], P(('col', 'rhs')), may hold values from 0 to 3, each once within a row
- sep_rhs: float32 [4096, 4096], P('rhs', 'col'), may hold values from -6 to 6
- factor_rows: bfloat16 [4096, 4096], P('col'), may hold values from -0.046875 to 0.046875
- diag_inverse: bfloat16 [4096, 1024], P('col'), may hold values from -1 to 1
Outputs:
- solved: float32 [4096, 4096], P('rhs', 'col')
The draws below stay inside these ranges and needn't reach their ends.
Inputs may be any that keep to these rules, and one draw needn't show every extreme that they name: `update_index`: within each group of 256 slots of a descendant the live entries come first and are distinct rows of the block that owner_map names for that group; the other slots hold -1. Every descendant has at least one group with all 256 slots live.
All inputs are finite; a program needn't handle non-finite values.
Results may differ from the reference program's by a relative error of at most 0.004.
Values sent between devices are 32-bit elements; how exact they have to be, the bound alone decides.
A program may use at most 128 MiB of HBM per device.

```python
import jax
import jax.numpy as jnp
from jax import lax

NB = 1024
CAP = 256
SEP = 4096
UPD = 1024
RHS_TOT = 4096
DESCS = 128
N_COL = 4


def draw_update_index(key, part):
    block_count = SEP // NB
    groups = DESCS * block_count
    group_keys = jax.random.split(key, groups)
    chosen = jax.vmap(lambda single: jax.random.permutation(single, NB)[:CAP])(group_keys)
    counts = jax.random.randint(jax.random.fold_in(key, 7), (DESCS, block_count), 1, CAP + 1)
    fullest = jax.random.randint(jax.random.fold_in(key, 11), (DESCS,), 0, block_count)
    counts = jnp.where(jnp.arange(block_count)[None, :] == fullest[:, None], CAP, counts)
    live_slots = jnp.arange(CAP)[None, None, :] < counts[:, :, None]
    result = jnp.where(live_slots, chosen.reshape(DESCS, block_count, CAP), -1)
    return result.reshape(DESCS, block_count * CAP).astype(jnp.int32)


def draw_diag_inverse(key, part):
    block_count = SEP // NB
    entries = jax.random.normal(key, (block_count, NB, NB), jnp.float32) * NB ** (-0.5)
    triangle = jnp.triu(entries, 1) + jnp.eye(NB, dtype=jnp.float32)[None, :, :]
    return triangle.reshape(block_count * NB, NB).astype(jnp.bfloat16)


def block_levels(key, shape, cuts, smallest, largest):
    loudness, own = 1.0, jax.random.fold_in(key, 6)
    for dim, parts in cuts:
        draws = jnp.exp(jax.random.uniform(jax.random.fold_in(own, dim), (parts,), jnp.float32, smallest / len(cuts), largest / len(cuts)))
        loudness = loudness * jnp.repeat(draws, shape[dim] // parts).reshape([-1 if axis == dim else 1 for axis in range(len(shape))])
    return loudness


def bell_draw(own_key, dims, scale, limit, shards=(), held_as=jnp.bfloat16):
    values = scale * jax.random.normal(own_key, dims, jnp.float32)
    if shards:
        values = values * block_levels(own_key, dims, shards, -0.22, 0.18)
    return jnp.clip(values, -limit, limit).astype(held_as)


def setup_inputs(seed: int = 0) -> dict:
    arg_keys = jax.random.split(jax.random.key(seed), 8)
    desc_rows = bell_draw(arg_keys[0], (DESCS, RHS_TOT, NB), 1.0, 6.0, ((0, 128),))
    upd_factor = bell_draw(arg_keys[1], (DESCS, NB, UPD), (32 * NB) ** -0.5, 0.03125, ((0, 128),))
    update_index = draw_update_index(jax.random.fold_in(arg_keys[7], 71), 0)
    owner_map = jax.vmap(lambda own: jax.random.permutation(own, N_COL))(jax.random.split(arg_keys[3], DESCS)).reshape((DESCS, N_COL)).astype(jnp.int32)
    sep_rhs = bell_draw(arg_keys[4], (RHS_TOT, SEP), 1.0, 6.0, ((0, 32), (1, 4)), jnp.float32)
    factor_rows = bell_draw(arg_keys[5], (SEP, SEP), (4 * SEP) ** -0.5, 0.046875, ((0, 4),))
    diag_inverse = draw_diag_inverse(jax.random.fold_in(arg_keys[7], 71), 0)
    return {"desc_rows": desc_rows, "upd_factor": upd_factor, "update_index": update_index, "owner_map": owner_map, "sep_rhs": sep_rhs, "factor_rows": factor_rows, "diag_inverse": diag_inverse}


def product(left, right):
    return jnp.dot(left.astype(jnp.float32), right.astype(jnp.float32),
                   precision=lax.Precision.HIGHEST, preferred_element_type=jnp.float32)


def reference(desc_rows, upd_factor, update_index, owner_map, sep_rhs, factor_rows, diag_inverse):
    def add_descendant(running, pieces):
        solved_rows, factor, local_index, owners = pieces
        update = product(solved_rows, factor)
        blocks = jnp.repeat(owners, CAP)
        targets = jnp.where(local_index >= 0, blocks * NB + local_index, SEP).astype(jnp.int32)
        return running.at[:, targets].add(update, mode="drop"), None

    assembled, _ = lax.scan(add_descendant, jnp.zeros((RHS_TOT, SEP), jnp.float32),
                            (desc_rows, upd_factor, update_index, owner_map))
    corrected = sep_rhs - assembled
    solved_blocks = []
    for column in range(N_COL):
        pending = jnp.zeros((RHS_TOT, NB), jnp.float32)
        for earlier in range(column):
            coupling = factor_rows[earlier * NB:(earlier + 1) * NB, column * NB:(column + 1) * NB]
            pending = pending + product(solved_blocks[earlier].astype(jnp.bfloat16), coupling)
        reduced = corrected[:, column * NB:(column + 1) * NB] - pending
        inverse_block = diag_inverse[column * NB:(column + 1) * NB]
        solved_blocks.append(product(reduced.astype(jnp.bfloat16), inverse_block))
    return jnp.concatenate(solved_blocks, axis=1)
```

```python
import functools

import jax
import jax.numpy as jnp
from jax import lax
from jax.experimental import pallas as pl
from jax.experimental.pallas import tpu as pltpu
from jax.sharding import PartitionSpec as P

MESH = pl.DeviceIdType.MESH
CHUNKS = 4
ORDERS = ((0, 2, 1), (2, 1, 0), (1, 0, 2), (0, 2, 1))


def flip(place, bit):
    low = place + 1 - 2 * lax.rem(place, 2)
    high = 3 - place
    return (1 - bit) * low + bit * high


def flip_if(place, bit, wanted):
    return place + wanted * (flip(place, bit) - place)


def kernel(owner, index, desc, factor, sep, rows_factor, inverse, out,
           left, fac_raw, fac, send, recv, index_send, index_recv, columns, onehot, wide,
           dense, half0, half1, half2, half3, base, corrected, pend_out, pend_in,
           load_sem, misc_sem, late_sem, index_ssem, index_rsem, s1_ssem, s1_rsem,
           h_ssem, h_rsem, p_ssem, p_rsem):
    block = inverse.shape[0]
    cap = index.shape[1] // 4
    tile = sep.shape[0]
    size = tile // CHUNKS
    halves = (half0, half1, half2, half3)

    z = lax.axis_index("col")
    rhs = lax.axis_index("rhs")
    core = lax.rem(rhs, 2)
    y = lax.rem(lax.div(rhs, 2), 4)
    x = lax.div(rhs, 8)
    star, rest = core, 1 - core

    def device(zz, yy, xx, kk):
        return (zz, (xx * 4 + yy) * 2 + kk)

    def other(kappa):
        return core + kappa * (1 - 2 * core)

    def star_peer(kappa, n):
        kk = other(kappa)
        return device(
            flip(z, kk) if n == 3 else z,
            flip(y, kk) if n == 2 else y,
            flip(x, kk) if n == 1 else x,
            kk,
        )

    def rest_peer(axis):
        return device(
            flip(z, rest) if axis == 0 else z,
            flip(y, rest) if axis == 1 else y,
            flip(x, rest) if axis == 2 else x,
            core,
        )

    antipode = device(flip(z, star), flip(y, star), flip(x, star), core)

    barrier = pltpu.get_barrier_semaphore()
    greeted = [device(z, y, x, 1 - core), antipode]
    for kk in (core, 1 - core):
        for bit in (0, 1):
            greeted.append(device(flip(z, bit), y, x, kk))
            greeted.append(device(z, flip(y, bit), x, kk))
            greeted.append(device(z, y, flip(x, bit), kk))
    greeted.append(device(lax.rem(z + 2, 4), y, x, core))
    for peer in greeted:
        pl.semaphore_signal(barrier, inc=1, device_id=peer, device_id_type=MESH)

    fac_copy = pltpu.make_async_copy(factor.at[0], fac_raw, misc_sem.at[0])
    fac_copy.start()
    for t in range(CHUNKS):
        def load(i, carry, t=t):
            kk = other(lax.div(i, 16))
            jx, jy = lax.rem(lax.div(i, 8), 2), lax.rem(lax.div(i, 4), 2)
            ry, rx = lax.rem(lax.div(i, 2), 2), lax.rem(i, 2)
            xx = flip_if(flip_if(x, kk, jx), 1 - kk, rx)
            yy = flip_if(flip_if(y, kk, jy), 1 - kk, ry)
            begin = ((xx * 4 + yy) * 2 + kk) * tile + t * size
            pltpu.make_async_copy(
                desc.at[0, pl.ds(pl.multiple_of(begin, size), size), :],
                left.at[t, pl.ds(pl.multiple_of(i * size, size), size), :],
                load_sem.at[t],
            ).start()
            return carry
        lax.fori_loop(0, 32, load, 0)
    base_copy = pltpu.make_async_copy(sep, base, misc_sem.at[1])
    base_copy.start()

    index_send[...] = jnp.full(index_send.shape, -1, jnp.int32)
    for blk in range(4):
        total = jnp.zeros((1, cap), jnp.int32)
        for g in range(4):
            total = total + index[0:1, g * cap : (g + 1) * cap] * (owner[0, g] == blk).astype(jnp.int32)
        index_send[blk : blk + 1, :] = total
    fac_copy.wait()

    def order_factor(i, carry):
        rows = pl.ds(pl.multiple_of(i * 128, 128), 128)
        for blk in range(4):
            total = fac_raw[rows, :cap]
            for g in range(1, 4):
                total = jnp.where(owner[0, g] == blk, fac_raw[rows, g * cap : (g + 1) * cap], total)
            fac[blk, rows, :] = total
        return carry

    lax.fori_loop(0, block // 128, order_factor, 0)

    def updates(t):
        slot = t % 2
        pltpu.make_async_copy(left.at[t], left.at[t], load_sem.at[t]).wait()

        def step(i, carry):
            kappa = 1 - lax.div(i, 4)
            dz0, dz1 = lax.rem(lax.div(i, 2), 2), lax.rem(i, 2)
            kk = other(kappa)
            zz = flip_if(flip_if(z, kk, dz0), 1 - kk, dz1)
            weights = fac[zz]
            for j, (n, a) in enumerate(((3 * dz0, 0), (2 - dz0, dz0), (1 + dz0, dz0), (3 - 3 * dz0, 1))):
                begin = (kappa * 16 + j * 4) * size
                rows = left[t, pl.ds(pl.multiple_of(begin, size), 4 * size), :]
                send[slot, kappa, n, a, dz1] = jnp.dot(
                    rows, weights, preferred_element_type=jnp.float32
                )
            return carry

        lax.fori_loop(0, 8, step, 0)

    def stage1(t, kappa, n):
        return pltpu.make_async_remote_copy(
            src_ref=send.at[t % 2, kappa, n],
            dst_ref=recv.at[t, kappa * 4 + n - 1],
            send_sem=s1_ssem.at[t % 2, kappa * 4 + n - 1],
            recv_sem=s1_rsem.at[t, kappa * 4 + n - 1],
            device_id=star_peer(kappa, n),
            device_id_type=MESH,
        )

    messages = [(1, 3), (1, 2), (1, 1), (0, 3), (0, 2), (0, 1), (1, 0)]

    def start_stage1(t):
        for kappa, n in messages:
            stage1(t, kappa, n).start()

    def index_copy(kappa, n):
        return pltpu.make_async_remote_copy(
            src_ref=index_send,
            dst_ref=index_recv.at[kappa * 4 + n],
            send_sem=index_ssem.at[kappa * 4 + n - 1],
            recv_sem=index_rsem.at[kappa * 4 + n - 1],
            device_id=star_peer(kappa, n),
            device_id_type=MESH,
        )

    def own_block(a, rz):
        return flip_if(flip_if(z, star, a), rest, rz)

    def index_columns():
        for kappa, n in messages:
            index_copy(kappa, n).wait()
        index_recv[0] = index_send[...]

        def step(i, carry):
            zz = own_block(lax.div(i, 2), lax.rem(i, 2))
            rows = [index_recv[m, pl.ds(zz, 1), :] for m in range(8)]
            rows = jnp.concatenate(rows + [jnp.full((120, cap), -1, jnp.int32)], axis=0)
            columns[i] = rows.T
            return carry

        lax.fori_loop(0, 4, step, 0)

    def assemble(t):
        for kappa, n in messages:
            stage1(t, kappa, n).wait_recv()

        def step(i, carry):
            a, rz = lax.div(i, 2), lax.rem(i, 2)
            listed = columns[i]
            lanes = lax.broadcasted_iota(jnp.int32, (cap, block), 1)
            for m in range(8):
                piece = send[t % 2, 0, 0, a, rz] if m == 0 else recv[t, m - 1, a, rz]
                wide[:, m * cap : (m + 1) * cap] = piece.astype(jnp.bfloat16)
                chosen = listed[:, m : m + 1] == lanes
                onehot[m * cap : (m + 1) * cap, :] = jnp.where(chosen, 1.0, 0.0).astype(jnp.bfloat16)
            total = jnp.dot(wide[...], onehot[...], preferred_element_type=jnp.float32)
            dense[t, a, rz] = total.reshape(2, 2, size, block)
            return carry

        lax.fori_loop(0, 4, step, 0)

    def part(t, stage, side):
        if stage == 3:
            return (t, side, 0, 0, 0)
        where = [slice(None)] * 3
        for axis in ORDERS[t][:stage]:
            where[axis] = 0
        where[ORDERS[t][stage]] = side
        return (t, slice(None), *where)

    def halving(t, stage):
        return pltpu.make_async_remote_copy(
            src_ref=dense.at[part(t, stage, 1)],
            dst_ref=halves[stage].at[t],
            send_sem=h_ssem.at[t, stage],
            recv_sem=h_rsem.at[t, stage],
            device_id=antipode if stage == 3 else rest_peer(ORDERS[t][stage]),
            device_id_type=MESH,
        )

    def add_half(t, stage):
        halving(t, stage).wait_recv()
        where = part(t, stage, 0)
        dense[where] = dense[where] + halves[stage][t]

    def first(t):
        assemble(t)
        halving(t, 0).start()

    def later(t, stage):
        add_half(t, stage - 1)
        halving(t, stage).start()

    def last(t):
        halving(t, 3).wait_recv()
        rows = slice(t * size, (t + 1) * size)
        corrected[rows, :] = base[rows, :] - (dense[t, 0, 0, 0, 0] + half3[t])

    def late_load(d):
        begin = pl.multiple_of((z + d) * block, block)
        return pltpu.make_async_copy(
            rows_factor.at[:, pl.ds(begin, block)], left.at[d - 1], late_sem.at[d]
        )

    inverse_load = pltpu.make_async_copy(inverse, left.at[3], late_sem.at[0])

    updates(0)
    pl.semaphore_wait(barrier, len(greeted))
    for kappa, n in messages:
        index_copy(kappa, n).start()
    start_stage1(0)
    updates(1)
    start_stage1(1)
    index_columns()
    first(0)
    for kappa, n in messages:
        stage1(0, kappa, n).wait_send()
    updates(2)
    start_stage1(2)
    first(1)
    later(0, 1)
    for kappa, n in messages:
        stage1(1, kappa, n).wait_send()
    updates(3)
    start_stage1(3)
    for d in range(1, 4):
        @pl.when(z + d < 4)
        def _(d=d):
            late_load(d).start()
    inverse_load.start()
    first(2)
    later(1, 1)
    later(0, 2)
    first(3)
    base_copy.wait()
    later(2, 1)
    later(1, 2)
    later(0, 3)
    later(3, 1)
    later(2, 2)
    later(1, 3)
    last(0)
    later(3, 2)
    later(2, 3)
    last(1)
    later(3, 3)
    last(2)
    last(3)
    for d in range(1, 4):
        @pl.when(z + d < 4)
        def _(d=d):
            late_load(d).wait()
    inverse_load.wait()

    def pending(station, d, t):
        rows = pl.ds(t * size, size)
        return pltpu.make_async_remote_copy(
            src_ref=pend_out.at[d - 1, rows, :],
            dst_ref=pend_in.at[station, rows, :],
            send_sem=p_ssem.at[d - 1, t],
            recv_sem=p_rsem.at[station, t],
            device_id=device(station + d, y, x, core),
            device_id_type=MESH,
        )

    for station in range(4):
        @pl.when(z == station)
        def _(station=station):
            for t in range(CHUNKS):
                rows = slice(t * size, (t + 1) * size)
                reduced = corrected[rows, :]
                for earlier in range(station):
                    pending(earlier, station - earlier, t).wait_recv()
                    reduced = reduced - pend_in[earlier, rows, :]
                solved = jnp.dot(
                    reduced.astype(jnp.bfloat16), left[3], preferred_element_type=jnp.float32
                )
                out[rows, :] = solved
                for d in range(1, 4 - station):
                    pend_out[d - 1, rows, :] = jnp.dot(
                        solved.astype(jnp.bfloat16), left[d - 1], preferred_element_type=jnp.float32
                    )
                    pending(station, d, t).start()
            for t in range(CHUNKS):
                for d in range(1, 4 - station):
                    pending(station, d, t).wait_send()

    for kappa, n in messages:
        stage1(2, kappa, n).wait_send()
        stage1(3, kappa, n).wait_send()
    for t in range(CHUNKS):
        for stage in range(4):
            halving(t, stage).wait_send()


def local(desc_rows, upd_factor, update_index, owner_map, sep_rhs, factor_rows, diag_inverse):
    tile, block = sep_rhs.shape
    cap = update_index.shape[1] // 4
    size = tile // CHUNKS
    f32, bf16, i32 = jnp.float32, jnp.bfloat16, jnp.int32
    vmem = pl.BlockSpec(memory_space=pltpu.VMEM)
    hbm = pl.BlockSpec(memory_space=pl.ANY)
    dma = pltpu.SemaphoreType.DMA
    return pl.pallas_call(
        kernel,
        out_shape=jax.ShapeDtypeStruct((tile, block), f32),
        in_specs=[pl.BlockSpec(memory_space=pltpu.SMEM), vmem, hbm, hbm, hbm, hbm, hbm],
        out_specs=vmem,
        scratch_shapes=[
            pltpu.VMEM((CHUNKS, 32 * size, block), bf16),
            pltpu.VMEM((block, 4 * cap), bf16),
            pltpu.VMEM((4, block, cap), bf16),
            pltpu.VMEM((2, 2, 4, 2, 2, 4 * size, cap), f32),
            pltpu.VMEM((CHUNKS, 7, 2, 2, 4 * size, cap), f32),
            pltpu.VMEM((8, cap), i32),
            pltpu.VMEM((8, 8, cap), i32),
            pltpu.VMEM((4, cap, 128), i32),
            pltpu.VMEM((8 * cap, block), bf16),
            pltpu.VMEM((4 * size, 8 * cap), bf16),
            pltpu.VMEM((CHUNKS, 2, 2, 2, 2, size, block), f32),
            pltpu.VMEM((CHUNKS, 2, 2, 2, size, block), f32),
            pltpu.VMEM((CHUNKS, 2, 2, size, block), f32),
            pltpu.VMEM((CHUNKS, 2, size, block), f32),
            pltpu.VMEM((CHUNKS, size, block), f32),
            pltpu.VMEM((tile, block), f32),
            pltpu.VMEM((tile, block), f32),
            pltpu.VMEM((3, tile, block), f32),
            pltpu.VMEM((3, tile, block), f32),
            dma((CHUNKS,)),
            dma((2,)),
            dma((4,)),
            dma((7,)),
            dma((7,)),
            dma((2, 7)),
            dma((CHUNKS, 7)),
            dma((CHUNKS, 4)),
            dma((CHUNKS, 4)),
            dma((3, CHUNKS)),
            dma((3, CHUNKS)),
        ],
        compiler_params=pltpu.CompilerParams(
            collective_id=0, has_side_effects=True, vmem_limit_bytes=67_000_000
        ),
    )(owner_map, update_index, desc_rows, upd_factor, sep_rhs, factor_rows, diag_inverse)


def solution(mesh):
    placed = (
        P(("col", "rhs"), None, None),
        P(("col", "rhs"), None, None),
        P(("col", "rhs"), None),
        P(("col", "rhs"), None),
        P("rhs", "col"),
        P("col", None),
        P("col", None),
    )
    return jax.shard_map(
        local, mesh=mesh, in_specs=placed, out_specs=P("rhs", "col"), check_vma=False
    )
```

```python
import functools

import jax
import jax.numpy as jnp
from jax import lax
from jax.experimental import pallas as pl
from jax.experimental.pallas import tpu as pltpu
from jax.sharding import PartitionSpec as P

MESH = pl.DeviceIdType.MESH
SIZES = (16, 32, 32, 32, 16)
STARTS = tuple(sum(SIZES[:t]) for t in range(len(SIZES)))
CHUNKS = len(SIZES)
SLOTS = 3
STRIPES = ((0, 384), (384, 384), (768, 256))
STEPS = (
    (0, 0), (0, 1), (1, 0), (0, 2), (1, 1), (0, 3), (2, 0), (1, 2),
    (0, 4), (2, 1), (1, 3), (3, 0), (2, 2), (1, 4), (3, 1), (2, 3),
    (4, 0), (3, 2), (2, 4), (5, 0), (4, 1), (3, 3), (4, 2), (3, 4),
    (4, 3), (5, 1), (4, 4), (5, 2), (5, 3), (5, 4),
)
LAGS = (0, 1, 2, 3)


def flip(place, bit):
    low = place + 1 - 2 * lax.rem(place, 2)
    high = 3 - place
    return (1 - bit) * low + bit * high


def flip_if(place, bit, wanted):
    return place + wanted * (flip(place, bit) - place)


def kernel(owner, index, desc, factor, sep, rows_factor, inverse, out,
           left, fac, own, index_send, index_recv, columns, onehot, wide, corrected, pend_in,
           load_sem, misc_sem, late_sem, index_ssem, index_rsem, s1_ssem, s1_rsem,
           h_ssem, h_rsem, a_ssem, a_rsem, p_ssem, p_rsem, *chunked):
    block = inverse.shape[0]
    cap = index.shape[1] // 4
    tile = sep.shape[0]
    send = chunked[:SLOTS]
    recv, dense, half0, half1, half2, half3 = (
        chunked[SLOTS + i * CHUNKS : SLOTS + (i + 1) * CHUNKS] for i in range(6)
    )
    halves = (half0, half1, half2)
    fac_raw = onehot.at[0:block]

    z = lax.axis_index("col")
    rhs = lax.axis_index("rhs")
    core = lax.rem(rhs, 2)
    y = lax.rem(lax.div(rhs, 2), 4)
    x = lax.div(rhs, 8)
    star, rest = core, 1 - core

    def device(zz, yy, xx, kk):
        return (zz, (xx * 4 + yy) * 2 + kk)

    def other(kappa):
        return core + kappa * (1 - 2 * core)

    def star_peer(kappa, n):
        kk = other(kappa)
        return device(
            flip(z, kk) if n == 3 else z,
            flip(y, kk) if n == 2 else y,
            flip(x, kk) if n == 1 else x,
            kk,
        )

    def rest_peer(axis):
        return device(
            flip(z, rest) if axis == 0 else z,
            flip(y, rest) if axis == 1 else y,
            flip(x, rest) if axis == 2 else x,
            core,
        )

    antipode = device(flip(z, star), flip(y, star), flip(x, star), core)

    barrier = pltpu.get_barrier_semaphore()
    greeted = [device(z, y, x, 1 - core), antipode]
    for kk in (core, 1 - core):
        for bit in (0, 1):
            greeted.append(device(flip(z, bit), y, x, kk))
            greeted.append(device(z, flip(y, bit), x, kk))
            greeted.append(device(z, y, flip(x, bit), kk))
    greeted.append(device(lax.rem(z + 2, 4), y, x, core))
    for peer in greeted:
        pl.semaphore_signal(barrier, inc=1, device_id=peer, device_id_type=MESH)

    fac_copy = pltpu.make_async_copy(factor.at[0], fac_raw, misc_sem.at[0])
    fac_copy.start()
    def load_rows(t):
        size = SIZES[t]

        def load(i, carry):
            kk = other(lax.div(i, 16))
            jx, jy = lax.rem(lax.div(i, 8), 2), lax.rem(lax.div(i, 4), 2)
            ry, rx = lax.rem(lax.div(i, 2), 2), lax.rem(i, 2)
            xx = flip_if(flip_if(x, kk, jx), 1 - kk, rx)
            yy = flip_if(flip_if(y, kk, jy), 1 - kk, ry)
            begin = ((xx * 4 + yy) * 2 + kk) * tile + STARTS[t]
            pltpu.make_async_copy(
                desc.at[0, pl.ds(pl.multiple_of(begin, 16), size), :],
                left.at[pl.ds(pl.multiple_of(32 * STARTS[t] + i * size, 16), size), :],
                load_sem.at[t],
            ).start()
            return carry

        lax.fori_loop(0, 32, load, 0)

    load_rows(0)
    base_copy = pltpu.make_async_copy(sep, corrected, misc_sem.at[1])

    index_send[...] = jnp.full(index_send.shape, -1, jnp.int32)
    for blk in range(4):
        total = jnp.zeros((1, cap), jnp.int32)
        for g in range(4):
            total = total + index[0:1, g * cap : (g + 1) * cap] * (owner[0, g] == blk).astype(jnp.int32)
        index_send[blk : blk + 1, :] = total
    fac_copy.wait()

    def order_factor(i, carry):
        rows = pl.ds(pl.multiple_of(i * 128, 128), 128)
        for blk in range(4):
            total = fac_raw[rows, :cap]
            for g in range(1, 4):
                total = jnp.where(owner[0, g] == blk, fac_raw[rows, g * cap : (g + 1) * cap], total)
            fac[blk, rows, :] = total
        return carry

    lax.fori_loop(0, block // 128, order_factor, 0)

    def updates(t):
        size, slot = SIZES[t], send[t % SLOTS]
        loaded = left.at[32 * STARTS[t] : 32 * (STARTS[t] + size)]
        pltpu.make_async_copy(loaded, loaded, load_sem.at[t]).wait()

        def step(i, carry):
            kappa = 1 - lax.div(i, 4)
            dz0, dz1 = lax.rem(lax.div(i, 2), 2), lax.rem(i, 2)
            kk = other(kappa)
            zz = flip_if(flip_if(z, kk, dz0), 1 - kk, dz1)
            weights = fac[zz]
            begin = pl.multiple_of(32 * STARTS[t] + kappa * 16 * size, 16)
            rows = left[pl.ds(begin, 16 * size), :]
            total = jnp.dot(rows, weights, preferred_element_type=jnp.float32)
            for j, (n, a) in enumerate(((3 * dz0, 0), (2 - dz0, dz0), (1 + dz0, dz0), (3 - 3 * dz0, 1))):
                slot[kappa, n, a, dz1, 0 : 4 * size] = total[j * 4 * size : (j + 1) * 4 * size]
            return carry

        lax.fori_loop(0, 4, step, 0)
        if t == 0:
            pl.semaphore_wait(barrier, len(greeted))
            for kappa, n in messages:
                index_copy(kappa, n).start()
        for kappa, n in messages:
            if kappa == 1:
                stage1(t, kappa, n).start()
        lax.fori_loop(4, 8, step, 0)
        for kappa, n in messages:
            if kappa == 0:
                stage1(t, kappa, n).start()
        for a in range(2):
            for rz in range(2):
                own[a, rz, 4 * STARTS[t] : 4 * (STARTS[t] + size), :] = (
                    slot[0, 0, a, rz, 0 : 4 * size, :].astype(jnp.bfloat16)
                )

    def stage1(t, kappa, n):
        return pltpu.make_async_remote_copy(
            src_ref=send[t % SLOTS].at[kappa, n, :, :, 0 : 4 * SIZES[t], :],
            dst_ref=recv[t].at[kappa * 4 + n - 1],
            send_sem=s1_ssem.at[t % SLOTS, kappa * 4 + n - 1],
            recv_sem=s1_rsem.at[t, kappa * 4 + n - 1],
            device_id=star_peer(kappa, n),
            device_id_type=MESH,
        )

    messages = [(1, 3), (1, 2), (1, 1), (0, 3), (0, 2), (0, 1), (1, 0)]

    def index_copy(kappa, n):
        return pltpu.make_async_remote_copy(
            src_ref=index_send,
            dst_ref=index_recv.at[kappa * 4 + n],
            send_sem=index_ssem.at[kappa * 4 + n - 1],
            recv_sem=index_rsem.at[kappa * 4 + n - 1],
            device_id=star_peer(kappa, n),
            device_id_type=MESH,
        )

    def own_block(a, rz):
        return flip_if(flip_if(z, star, a), rest, rz)

    def index_columns():
        for kappa, n in messages:
            index_copy(kappa, n).wait()
        index_recv[0] = index_send[...]

        def step(i, carry):
            zz = own_block(lax.div(i, 2), lax.rem(i, 2))
            rows = [index_recv[m, pl.ds(zz, 1), :] for m in range(8)]
            rows = jnp.concatenate(rows + [jnp.full((120, cap), -1, jnp.int32)], axis=0)
            columns[i] = rows.T.astype(jnp.int16)
            return carry

        lax.fori_loop(0, 4, step, 0)

    def assemble(t):
        size = SIZES[t]
        for kappa, n in messages:
            stage1(t, kappa, n).wait_recv()

        def step(i, carry):
            a, rz = lax.div(i, 2), lax.rem(i, 2)
            listed = columns[i]
            lanes = lax.broadcasted_iota(jnp.int32, (cap, block), 1).astype(jnp.int16)
            one, zero = jnp.bfloat16(1), jnp.bfloat16(0)
            for m in range(8):
                if m == 0:
                    piece = own[a, rz, 4 * STARTS[t] : 4 * (STARTS[t] + size), :]
                else:
                    piece = recv[t][m - 1, a, rz].astype(jnp.bfloat16)
                wide[0 : 4 * size, m * cap : (m + 1) * cap] = piece
                chosen = listed[:, m : m + 1] == lanes
                onehot[m * cap : (m + 1) * cap, :] = jnp.where(chosen, one, zero)
            total = jnp.dot(
                wide[0 : 4 * size, :], onehot[...], preferred_element_type=jnp.float32
            )
            dense[t][a, rz] = total.reshape(2, 2, size, block)
            return carry

        lax.fori_loop(0, 4, step, 0)

    def rows_of(t):
        return slice(STARTS[t], STARTS[t] + SIZES[t])

    def axis_of(t, stripe, stage):
        return (t + stripe + stage) % 3

    def part(t, stripe, stage, side):
        where = [slice(None)] * 3
        for before in range(stage):
            where[axis_of(t, stripe, before)] = 0
        where[axis_of(t, stripe, stage)] = side
        begin, width = STRIPES[stripe]
        return (slice(None), *where, slice(None), slice(begin, begin + width))

    def landing(stripe, stage):
        begin, width = STRIPES[stripe]
        return (*[slice(None)] * (4 - stage), slice(begin, begin + width))

    def halving(t, stripe, stage):
        return pltpu.make_async_remote_copy(
            src_ref=dense[t].at[part(t, stripe, stage, 1)],
            dst_ref=halves[stage][t].at[landing(stripe, stage)],
            send_sem=h_ssem.at[t, stage, stripe],
            recv_sem=h_rsem.at[t, stage, stripe],
            device_id=rest_peer(axis_of(t, stripe, stage)),
            device_id_type=MESH,
        )

    def crossing(t):
        return pltpu.make_async_remote_copy(
            src_ref=dense[t].at[1, 0, 0, 0],
            dst_ref=half3[t],
            send_sem=a_ssem.at[t],
            recv_sem=a_rsem.at[t],
            device_id=antipode,
            device_id_type=MESH,
        )

    def first(t):
        assemble(t)
        for stripe in range(3):
            halving(t, stripe, 0).start()

    def later(t, stage):
        for stripe in range(3):
            halving(t, stripe, stage - 1).wait_recv()
            where = part(t, stripe, stage - 1, 0)
            dense[t][where] = dense[t][where] + halves[stage - 1][t][landing(stripe, stage - 1)]
            if stage < 3:
                halving(t, stripe, stage).start()
        if stage == 3:
            crossing(t).start()

    def last(t):
        crossing(t).wait_recv()
        rows = rows_of(t)
        corrected[rows, :] = corrected[rows, :] - (dense[t][0, 0, 0, 0] + half3[t][...])

    def late_load(d):
        begin = pl.multiple_of((z + d) * block, block)
        return pltpu.make_async_copy(
            rows_factor.at[:, pl.ds(begin, block)], left.at[(d - 1) * block : d * block], late_sem.at[d]
        )

    inverse_load = pltpu.make_async_copy(inverse, left.at[3 * block : 4 * block], late_sem.at[0])

    def pending(station, d, t):
        rows = pl.ds(t * size, size)
        return pltpu.make_async_remote_copy(
            src_ref=pend_out.at[d - 1, rows, :],
            dst_ref=pend_in.at[station, rows, :],
            send_sem=p_ssem.at[d - 1, t],
            recv_sem=p_rsem.at[station, t],
            device_id=device(station + d, y, x, core),
            device_id_type=MESH,
        )

    def solve(station, t):
        rows = slice(t * size, (t + 1) * size)
        reduced = corrected[rows, :]
        for earlier in range(station):
            pending(earlier, station - earlier, t).wait_recv()
            reduced = reduced - pend_in[earlier, rows, :]
        solved = jnp.dot(
            reduced.astype(jnp.bfloat16), left[3], preferred_element_type=jnp.float32
        )
        out[rows, :] = solved
        for d in range(1, 4 - station):
            pend_out[d - 1, rows, :] = jnp.dot(
                solved.astype(jnp.bfloat16), left[d - 1], preferred_element_type=jnp.float32
            )
            pending(station, d, t).start()

    def solve_after(t):
        for station in range(4):
            chunks = [t - station] if t < CHUNKS - 1 else range(max(0, t - station), CHUNKS)
            if t - station >= 0 or t == CHUNKS - 1:
                @pl.when(z == station)
                def _(station=station, chunks=chunks):
                    for chunk in chunks:
                        solve(station, chunk)

    def pending(station, d, t):
        return pltpu.make_async_remote_copy(
            src_ref=half0[t].at[(0, d // 3, (d - 1) % 2)],
            dst_ref=pend_in.at[station, rows_of(t), :],
            send_sem=p_ssem.at[d - 1, t],
            recv_sem=p_rsem.at[station, t],
            device_id=device(station + d, y, x, core),
            device_id_type=MESH,
        )

    def spread(station, d, t, solved):
        half0[t][0, d // 3, (d - 1) % 2] = jnp.dot(
            solved.astype(jnp.bfloat16),
            left[(d - 1) * block : d * block, :],
            preferred_element_type=jnp.float32,
        )
        pending(station, d, t).start()

    def solve(station, t):
        rows = rows_of(t)
        reduced = corrected[rows, :]
        for earlier in range(station):
            pending(earlier, station - earlier, t).wait_recv()
            reduced = reduced - pend_in[earlier, rows, :]
        solved = jnp.dot(
            reduced.astype(jnp.bfloat16),
            left[3 * block : 4 * block, :],
            preferred_element_type=jnp.float32,
        )
        out[rows, :] = solved
        if station < 3:
            spread(station, 1, t, solved)
        for before in ([t - 1] if t else []) + ([t] if t == CHUNKS - 1 else []):
            for d in range(2, 4 - station):
                spread(station, d, before, out[rows_of(before), :])

    def solve_after(t):
        for station in range(4):
            lag = LAGS[station]
            chunks = [t - lag] if t < CHUNKS - 1 else list(range(max(0, t - lag), CHUNKS))
            if t - lag >= 0 or t == CHUNKS - 1:
                @pl.when(z == station)
                def _(station=station, chunks=chunks):
                    for chunk in chunks:
                        solve(station, chunk)

    def finish(t):
        last(t)
        solve_after(t)

    def products(t):
        if t + 1 < CHUNKS:
            load_rows(t + 1)
        if t >= SLOTS:
            for kappa, n in messages:
                stage1(t - SLOTS, kappa, n).wait_send()
        updates(t)
        if t == 1:
            base_copy.start()
        if t == CHUNKS - 1:
            for d in range(1, 4):
                @pl.when(z + d < 4)
                def _(d=d):
                    late_load(d).start()
            inverse_load.start()

    crossed = []
    for name, t in STEPS:
        if name == 0:
            products(t)
        elif name == 1:
            if t == 0:
                index_columns()
            first(t)
        elif name < 5:
            later(t, name - 1)
        else:
            if not crossed:
                for d in range(1, 4):
                    @pl.when(z + d < 4)
                    def _(d=d):
                        late_load(d).wait()
                inverse_load.wait()
                base_copy.wait()
            crossed.append(t)
            finish(t)

    for station in range(3):
        @pl.when(z == station)
        def _(station=station):
            for t in range(CHUNKS):
                for d in range(1, 4 - station):
                    pending(station, d, t).wait_send()
    for kappa, n in messages:
        for t in range(max(0, CHUNKS - SLOTS), CHUNKS):
            stage1(t, kappa, n).wait_send()
    for t in range(CHUNKS):
        for stripe in range(3):
            for stage in range(3):
                halving(t, stripe, stage).wait_send()
        crossing(t).wait_send()


def local(desc_rows, upd_factor, update_index, owner_map, sep_rhs, factor_rows, diag_inverse):
    tile, block = sep_rhs.shape
    cap = update_index.shape[1] // 4
    f32, bf16, i32 = jnp.float32, jnp.bfloat16, jnp.int32
    vmem = pl.BlockSpec(memory_space=pltpu.VMEM)
    hbm = pl.BlockSpec(memory_space=pl.ANY)
    dma = pltpu.SemaphoreType.DMA
    most = max(SIZES)
    chunked = [pltpu.VMEM((2, 4, 2, 2, 4 * most, cap), f32) for _ in range(SLOTS)]
    for lead in ((7, 2, 2, 4), (2, 2, 2, 2), (2, 2, 2), (2, 2), (2,), ()):
        for size in SIZES:
            if len(lead) == 4 and lead[0] == 7:
                chunked.append(pltpu.VMEM((7, 2, 2, 4 * size, cap), f32))
            else:
                chunked.append(pltpu.VMEM((*lead, size, block), f32))
    return pl.pallas_call(
        kernel,
        out_shape=jax.ShapeDtypeStruct((tile, block), f32),
        in_specs=[pl.BlockSpec(memory_space=pltpu.SMEM), vmem, hbm, hbm, hbm, hbm, hbm],
        out_specs=vmem,
        scratch_shapes=[
            pltpu.VMEM((32 * tile, block), bf16),
            pltpu.VMEM((4, block, cap), bf16),
            pltpu.VMEM((2, 2, 4 * tile, cap), bf16),
            pltpu.VMEM((8, cap), i32),
            pltpu.VMEM((8, 8, cap), i32),
            pltpu.VMEM((4, cap, 128), jnp.int16),
            pltpu.VMEM((8 * cap, block), bf16),
            pltpu.VMEM((4 * most, 8 * cap), bf16),
            pltpu.VMEM((tile, block), f32),
            pltpu.VMEM((3, tile, block), f32),
            dma((CHUNKS,)),
            dma((2,)),
            dma((4,)),
            dma((7,)),
            dma((7,)),
            dma((SLOTS, 7)),
            dma((CHUNKS, 7)),
            dma((CHUNKS, 3, 3)),
            dma((CHUNKS, 3, 3)),
            dma((CHUNKS,)),
            dma((CHUNKS,)),
            dma((3, CHUNKS)),
            dma((3, CHUNKS)),
            *chunked,
        ],
        compiler_params=pltpu.CompilerParams(
            collective_id=0, has_side_effects=True, vmem_limit_bytes=67_000_000
        ),
    )(owner_map, update_index, desc_rows, upd_factor, sep_rhs, factor_rows, diag_inverse)


def solution(mesh):
    placed = (
        P(("col", "rhs"), None, None),
        P(("col", "rhs"), None, None),
        P(("col", "rhs"), None),
        P(("col", "rhs"), None),
        P("rhs", "col"),
        P("col", None),
        P("col", None),
    )
    return jax.shard_map(
        local, mesh=mesh, in_specs=placed, out_specs=P("rhs", "col"), check_vma=False
    )
```

```python
import functools

import jax
import jax.numpy as jnp
from jax import lax
from jax.experimental import pallas as pl
from jax.experimental.pallas import tpu as pltpu
from jax.sharding import PartitionSpec as P

MESH = pl.DeviceIdType.MESH
SIZES = (16, 32, 32, 32, 16)
STARTS = tuple(sum(SIZES[:t]) for t in range(len(SIZES)))
CHUNKS = len(SIZES)
SLOTS = 3
STRIPES = ((0, 384), (384, 384), (768, 256))
AXES = tuple(tuple(tuple((t + i + j) % 3 for j in range(3)) for i in range(3)) for t in range(3))
STEPS = (
    (0, 0), (0, 1), (1, 0), (0, 2), (2, 0), (0, 3), (3, 0), (1, 2),
    (0, 4), (1, 1), (2, 2), (1, 3), (4, 0), (2, 1), (1, 4), (5, 0),
    (3, 2), (3, 1), (2, 3), (4, 1), (2, 4), (3, 3), (3, 4), (4, 2),
    (4, 3), (5, 1), (6, 0), (5, 2), (6, 1), (7, 0), (4, 4), (5, 3),
    (6, 2), (7, 1), (8, 0), (5, 4), (6, 3), (7, 2), (8, 1), (6, 4),
    (7, 3), (8, 2), (7, 4), (8, 3), (8, 4),
)


def flip(place, bit):
    low = place + 1 - 2 * lax.rem(place, 2)
    high = 3 - place
    return (1 - bit) * low + bit * high


def flip_if(place, bit, wanted):
    return place + wanted * (flip(place, bit) - place)


def kernel(owner, index, desc, factor, sep, rows_factor, inverse, out_hbm,
           left, fac, own, index_send, index_recv, columns, onehot, wide, corrected, out, pend_in,
           load_sem, misc_sem, late_sem, index_ssem, index_rsem, s1_ssem, s1_rsem,
           h_ssem, h_rsem, a_ssem, a_rsem, p_ssem, p_rsem, out_sem, *chunked):
    block = inverse.shape[0]
    cap = index.shape[1] // 4
    tile = sep.shape[0]
    send = chunked[:SLOTS]
    recv, dense, half0, half1, half2, half3 = (
        chunked[SLOTS + i * CHUNKS : SLOTS + (i + 1) * CHUNKS] for i in range(6)
    )
    halves = (half0, half1, half2)
    fac_raw = onehot.at[0:block]

    z = lax.axis_index("col")
    rhs = lax.axis_index("rhs")
    core = lax.rem(rhs, 2)
    y = lax.rem(lax.div(rhs, 2), 4)
    x = lax.div(rhs, 8)
    star, rest = core, 1 - core

    def device(zz, yy, xx, kk):
        return (zz, (xx * 4 + yy) * 2 + kk)

    def other(kappa):
        return core + kappa * (1 - 2 * core)

    def star_peer(kappa, n):
        kk = other(kappa)
        return device(
            flip(z, kk) if n == 3 else z,
            flip(y, kk) if n == 2 else y,
            flip(x, kk) if n == 1 else x,
            kk,
        )

    def rest_peer(axis):
        return device(
            flip(z, rest) if axis == 0 else z,
            flip(y, rest) if axis == 1 else y,
            flip(x, rest) if axis == 2 else x,
            core,
        )

    antipode = device(flip(z, star), flip(y, star), flip(x, star), core)

    fac_copy = pltpu.make_async_copy(factor.at[0], fac_raw, misc_sem.at[0])
    fac_copy.start()

    barrier = pltpu.get_barrier_semaphore()
    greeted = [device(z, y, x, 1 - core), antipode]
    for kk in (core, 1 - core):
        for bit in (0, 1):
            greeted.append(device(flip(z, bit), y, x, kk))
            greeted.append(device(z, flip(y, bit), x, kk))
            greeted.append(device(z, y, flip(x, bit), kk))
    greeted.append(device(lax.rem(z + 2, 4), y, x, core))
    for peer in greeted:
        pl.semaphore_signal(barrier, inc=1, device_id=peer, device_id_type=MESH)

    def load_rows(t):
        size = SIZES[t]

        def load(i, carry):
            kk = other(lax.div(i, 16))
            jx, jy = lax.rem(lax.div(i, 8), 2), lax.rem(lax.div(i, 4), 2)
            ry, rx = lax.rem(lax.div(i, 2), 2), lax.rem(i, 2)
            xx = flip_if(flip_if(x, kk, jx), 1 - kk, rx)
            yy = flip_if(flip_if(y, kk, jy), 1 - kk, ry)
            begin = ((xx * 4 + yy) * 2 + kk) * tile + STARTS[t]
            pltpu.make_async_copy(
                desc.at[0, pl.ds(pl.multiple_of(begin, 16), size), :],
                left.at[pl.ds(pl.multiple_of(32 * STARTS[t] + i * size, 16), size), :],
                load_sem.at[t],
            ).start()
            return carry

        lax.fori_loop(0, 32, load, 0)

    load_rows(0)
    base_copy = pltpu.make_async_copy(sep, corrected, misc_sem.at[1])

    index_send[...] = jnp.full(index_send.shape, -1, jnp.int32)
    for blk in range(4):
        total = jnp.zeros((1, cap), jnp.int32)
        for g in range(4):
            total = total + index[0:1, g * cap : (g + 1) * cap] * (owner[0, g] == blk).astype(jnp.int32)
        index_send[blk : blk + 1, :] = total
    fac_copy.wait()

    def order_factor(i, carry):
        rows = pl.ds(pl.multiple_of(i * 128, 128), 128)
        for blk in range(4):
            total = fac_raw[rows, :cap]
            for g in range(1, 4):
                total = jnp.where(owner[0, g] == blk, fac_raw[rows, g * cap : (g + 1) * cap], total)
            fac[blk, rows, :] = total
        return carry

    lax.fori_loop(0, block // 128, order_factor, 0)

    def updates(t):
        size, slot = SIZES[t], send[t % SLOTS]
        loaded = left.at[32 * STARTS[t] : 32 * (STARTS[t] + size)]
        pltpu.make_async_copy(loaded, loaded, load_sem.at[t]).wait()

        def step(i, carry):
            kappa = 1 - lax.div(i, 4)
            dz0, dz1 = lax.rem(lax.div(i, 2), 2), lax.rem(i, 2)
            kk = other(kappa)
            zz = flip_if(flip_if(z, kk, dz0), 1 - kk, dz1)
            weights = fac[zz]
            begin = pl.multiple_of(32 * STARTS[t] + kappa * 16 * size, 16)
            rows = left[pl.ds(begin, 16 * size), :]
            total = jnp.dot(rows, weights, preferred_element_type=jnp.float32)
            for j, (n, a) in enumerate(((3 * dz0, 0), (2 - dz0, dz0), (1 + dz0, dz0), (3 - 3 * dz0, 1))):
                slot[kappa, n, a, dz1, 0 : 4 * size] = total[j * 4 * size : (j + 1) * 4 * size]
            return carry

        lax.fori_loop(0, 4, step, 0)
        if t == 0:
            pl.semaphore_wait(barrier, len(greeted))
            for kappa, n in messages:
                index_copy(kappa, n).start()
        for kappa, n in messages:
            if kappa == 1:
                stage1(t, kappa, n).start()
        if t + 1 < CHUNKS:
            load_rows(t + 1)
        lax.fori_loop(4, 8, step, 0)
        for kappa, n in messages:
            if kappa == 0:
                stage1(t, kappa, n).start()
        for a in range(2):
            for rz in range(2):
                own[a, rz, 4 * STARTS[t] : 4 * (STARTS[t] + size), :] = (
                    slot[0, 0, a, rz, 0 : 4 * size, :].astype(jnp.bfloat16)
                )

    def stage1(t, kappa, n):
        return pltpu.make_async_remote_copy(
            src_ref=send[t % SLOTS].at[kappa, n, :, :, 0 : 4 * SIZES[t], :],
            dst_ref=recv[t].at[kappa * 4 + n - 1],
            send_sem=s1_ssem.at[t % SLOTS, kappa * 4 + n - 1],
            recv_sem=s1_rsem.at[t, kappa * 4 + n - 1],
            device_id=star_peer(kappa, n),
            device_id_type=MESH,
        )

    messages = [(1, 3), (1, 2), (1, 1), (0, 3), (0, 2), (0, 1), (1, 0)]

    def index_copy(kappa, n):
        return pltpu.make_async_remote_copy(
            src_ref=index_send,
            dst_ref=index_recv.at[kappa * 4 + n],
            send_sem=index_ssem.at[kappa * 4 + n - 1],
            recv_sem=index_rsem.at[kappa * 4 + n - 1],
            device_id=star_peer(kappa, n),
            device_id_type=MESH,
        )

    def own_block(a, rz):
        return flip_if(flip_if(z, star, a), rest, rz)

    def index_columns():
        for kappa, n in messages:
            index_copy(kappa, n).wait()
        index_recv[0] = index_send[...]

        def step(i, carry):
            zz = own_block(lax.div(i, 2), lax.rem(i, 2))
            rows = [index_recv[m, pl.ds(zz, 1), :] for m in range(8)]
            rows = jnp.concatenate(rows + [jnp.full((120, cap), -1, jnp.int32)], axis=0)
            columns[i] = rows.T.astype(jnp.int16)
            return carry

        lax.fori_loop(0, 4, step, 0)

    def assemble(t):
        size = SIZES[t]
        for kappa, n in messages:
            stage1(t, kappa, n).wait_recv()

        def step(i, carry):
            a, rz = lax.div(i, 2), lax.rem(i, 2)
            listed = columns[i]
            lanes = lax.broadcasted_iota(jnp.int32, (cap, block), 1).astype(jnp.int16)
            one, zero = jnp.bfloat16(1), jnp.bfloat16(0)
            for m in range(8):
                if m == 0:
                    piece = own[a, rz, 4 * STARTS[t] : 4 * (STARTS[t] + size), :]
                else:
                    piece = recv[t][m - 1, a, rz].astype(jnp.bfloat16)
                wide[0 : 4 * size, m * cap : (m + 1) * cap] = piece
                chosen = listed[:, m : m + 1] == lanes
                onehot[m * cap : (m + 1) * cap, :] = jnp.where(chosen, one, zero)
            total = jnp.dot(
                wide[0 : 4 * size, :], onehot[...], preferred_element_type=jnp.float32
            )
            dense[t][a, rz] = total.reshape(2, 2, size, block)
            return carry

        lax.fori_loop(0, 4, step, 0)

    def rows_of(t):
        return slice(STARTS[t], STARTS[t] + SIZES[t])

    def axis_of(t, stripe, stage):
        return AXES[t % len(AXES)][stripe][stage]

    def part(t, stripe, stage, side):
        where = [slice(None)] * 3
        for before in range(stage):
            where[axis_of(t, stripe, before)] = 0
        where[axis_of(t, stripe, stage)] = side
        begin, width = STRIPES[stripe]
        return (slice(None), *where, slice(None), slice(begin, begin + width))

    def landing(stripe, stage):
        begin, width = STRIPES[stripe]
        return (*[slice(None)] * (4 - stage), slice(begin, begin + width))

    def halving(t, stripe, stage):
        return pltpu.make_async_remote_copy(
            src_ref=dense[t].at[part(t, stripe, stage, 1)],
            dst_ref=halves[stage][t].at[landing(stripe, stage)],
            send_sem=h_ssem.at[t, stage, stripe],
            recv_sem=h_rsem.at[t, stage, stripe],
            device_id=rest_peer(axis_of(t, stripe, stage)),
            device_id_type=MESH,
        )

    def crossing(t):
        return pltpu.make_async_remote_copy(
            src_ref=dense[t].at[1, 0, 0, 0],
            dst_ref=half3[t],
            send_sem=a_ssem.at[t],
            recv_sem=a_rsem.at[t],
            device_id=antipode,
            device_id_type=MESH,
        )

    def first(t):
        assemble(t)
        for stripe in range(3):
            halving(t, stripe, 0).start()

    def later(t, stage):
        for stripe in range(3):
            halving(t, stripe, stage - 1).wait_recv()
            where = part(t, stripe, stage - 1, 0)
            dense[t][where] = dense[t][where] + halves[stage - 1][t][landing(stripe, stage - 1)]
            if stage < 3:
                halving(t, stripe, stage).start()
        if stage == 3:
            crossing(t).start()

    def last(t):
        crossing(t).wait_recv()
        rows = rows_of(t)
        corrected[rows, :] = corrected[rows, :] - (dense[t][0, 0, 0, 0] + half3[t][...])

    def late_load(d):
        begin = pl.multiple_of((z + d) * block, block)
        return pltpu.make_async_copy(
            rows_factor.at[:, pl.ds(begin, block)], left.at[(d - 1) * block : d * block], late_sem.at[d]
        )

    inverse_load = pltpu.make_async_copy(inverse, left.at[3 * block : 4 * block], late_sem.at[0])

    def pending(station, d, t):
        return pltpu.make_async_remote_copy(
            src_ref=half0[t].at[(0, d // 3, (d - 1) % 2)],
            dst_ref=pend_in.at[station, rows_of(t), :],
            send_sem=p_ssem.at[d - 1, t],
            recv_sem=p_rsem.at[station, t],
            device_id=device(station + d, y, x, core),
            device_id_type=MESH,
        )

    def spread(station, d, t, solved):
        half0[t][0, d // 3, (d - 1) % 2] = jnp.dot(
            solved.astype(jnp.bfloat16),
            left[(d - 1) * block : d * block, :],
            preferred_element_type=jnp.float32,
        )
        pending(station, d, t).start()

    def out_copy(t):
        rows = rows_of(t)
        return pltpu.make_async_copy(out.at[rows, :], out_hbm.at[rows, :], out_sem.at[t])

    def solve(station, t):
        rows = rows_of(t)
        reduced = corrected[rows, :]
        for earlier in range(station):
            pending(earlier, station - earlier, t).wait_recv()
            reduced = reduced - pend_in[earlier, rows, :]
        solved = jnp.dot(
            reduced.astype(jnp.bfloat16),
            left[3 * block : 4 * block, :],
            preferred_element_type=jnp.float32,
        )
        out[rows, :] = solved
        out_copy(t).start()
        if station < 3:
            spread(station, 1, t, solved)
        for before in ([t - 1] if t else []) + ([t] if t == CHUNKS - 1 else []):
            for d in range(2, 4 - station):
                spread(station, d, before, out[rows_of(before), :])

    def station_solve(station, t):
        @pl.when(z == station)
        def _():
            solve(station, t)

    def finish(t):
        last(t)
        station_solve(0, t)

    def products(t):
        if t >= SLOTS:
            for kappa, n in messages:
                stage1(t - SLOTS, kappa, n).wait_send()
        updates(t)
        if t == 1:
            base_copy.start()
        if t == CHUNKS - 1:
            for d in range(1, 4):
                @pl.when(z + d < 4)
                def _(d=d):
                    late_load(d).start()
            inverse_load.start()

    crossed = []
    for name, t in STEPS:
        if name == 0:
            products(t)
        elif name == 1:
            if t == 0:
                index_columns()
            first(t)
        elif name < 5:
            later(t, name - 1)
        elif name > 5:
            station_solve(name - 5, t)
        else:
            if not crossed:
                for d in range(1, 4):
                    @pl.when(z + d < 4)
                    def _(d=d):
                        late_load(d).wait()
                inverse_load.wait()
                base_copy.wait()
            crossed.append(t)
            finish(t)

    for station in range(3):
        @pl.when(z == station)
        def _(station=station):
            for t in range(CHUNKS):
                for d in range(1, 4 - station):
                    pending(station, d, t).wait_send()
    for kappa, n in messages:
        for t in range(max(0, CHUNKS - SLOTS), CHUNKS):
            stage1(t, kappa, n).wait_send()
    for t in range(CHUNKS):
        out_copy(t).wait()
        for stripe in range(3):
            for stage in range(3):
                halving(t, stripe, stage).wait_send()
        crossing(t).wait_send()


def local(desc_rows, upd_factor, update_index, owner_map, sep_rhs, factor_rows, diag_inverse):
    tile, block = sep_rhs.shape
    cap = update_index.shape[1] // 4
    f32, bf16, i32 = jnp.float32, jnp.bfloat16, jnp.int32
    vmem = pl.BlockSpec(memory_space=pltpu.VMEM)
    hbm = pl.BlockSpec(memory_space=pl.ANY)
    dma = pltpu.SemaphoreType.DMA
    most = max(SIZES)
    chunked = [pltpu.VMEM((2, 4, 2, 2, 4 * most, cap), f32) for _ in range(SLOTS)]
    for lead in ((7, 2, 2, 4), (2, 2, 2, 2), (2, 2, 2), (2, 2), (2,), ()):
        for size in SIZES:
            if len(lead) == 4 and lead[0] == 7:
                chunked.append(pltpu.VMEM((7, 2, 2, 4 * size, cap), f32))
            else:
                chunked.append(pltpu.VMEM((*lead, size, block), f32))
    return pl.pallas_call(
        kernel,
        out_shape=jax.ShapeDtypeStruct((tile, block), f32),
        in_specs=[pl.BlockSpec(memory_space=pltpu.SMEM), vmem, hbm, hbm, hbm, hbm, hbm],
        out_specs=hbm,
        scratch_shapes=[
            pltpu.VMEM((32 * tile, block), bf16),
            pltpu.VMEM((4, block, cap), bf16),
            pltpu.VMEM((2, 2, 4 * tile, cap), bf16),
            pltpu.VMEM((8, cap), i32),
            pltpu.VMEM((8, 8, cap), i32),
            pltpu.VMEM((4, cap, 128), jnp.int16),
            pltpu.VMEM((8 * cap, block), bf16),
            pltpu.VMEM((4 * most, 8 * cap), bf16),
            pltpu.VMEM((tile, block), f32),
            pltpu.VMEM((tile, block), f32),
            pltpu.VMEM((3, tile, block), f32),
            dma((CHUNKS,)),
            dma((2,)),
            dma((4,)),
            dma((7,)),
            dma((7,)),
            dma((SLOTS, 7)),
            dma((CHUNKS, 7)),
            dma((CHUNKS, 3, 3)),
            dma((CHUNKS, 3, 3)),
            dma((CHUNKS,)),
            dma((CHUNKS,)),
            dma((3, CHUNKS)),
            dma((3, CHUNKS)),
            dma((CHUNKS,)),
            *chunked,
        ],
        compiler_params=pltpu.CompilerParams(
            collective_id=0, has_side_effects=True, vmem_limit_bytes=65_000_000
        ),
    )(owner_map, update_index, desc_rows, upd_factor, sep_rhs, factor_rows, diag_inverse)


def solution(mesh):
    placed = (
        P(("col", "rhs"), None, None),
        P(("col", "rhs"), None, None),
        P(("col", "rhs"), None),
        P(("col", "rhs"), None),
        P("rhs", "col"),
        P("col", None),
        P("col", None),
    )
    return jax.shard_map(
        local, mesh=mesh, in_specs=placed, out_specs=P("rhs", "col"), check_vma=False
    )
```
